32 devices in a mesh: gx: 2 (over y), gy: 4 (over z), gz: 4 (over x, core).
Axes of the slice: x: 2, y: 2, z: 4, core: 2. Of those that a mesh axis runs over, the one named last changes fastest.
Arguments:
- field: float32 [4, 512, 16, 512], P('gx', 'gy', None, 'gz'), may hold values from -45 to 45
- start_basis: float32 [512, 128], replicated, may hold values from -6 to 6
Outputs:
- factor_out: float32 [512, 512], P('gy', 'gz')
- core: float32 [4, 128, 16, 512], P('gx', 'gy', None, 'gz')
The draws below stay inside these ranges and needn't reach their ends.
All inputs are finite; a program needn't handle non-finite values.
Results may differ from the reference program's by a relative error of at most 0.0003.
Values sent between devices are 32-bit elements; how exact they have to be, the bound alone decides.
A program may use at most 64 MiB of HBM per device.

```python
import jax
import jax.numpy as jnp
from jax import lax

NY = 512
RANK = 128
NS = 16
ITERS = 2
NX = 4
NZ = 512


def draw_field(key, part):
    keys = jax.random.split(key, 2)
    planes = jnp.arange(NX, dtype=jnp.float32)
    rising = 3.0 ** (planes / max(NX - 1, 1))
    plane_scale = jnp.exp(jax.random.uniform(keys[0], (NX, NY, NS, 1), jnp.float32) * jnp.log(10.0))
    plane_scale = plane_scale * rising[:, None, None, None] * 0.25
    shape = (NX, NY, NS, NZ)
    values = plane_scale * jnp.clip(jax.random.normal(keys[1], shape, jnp.float32), -6.0, 6.0)
    return values


def scatter_about(key, dims, scale, most, kind=jnp.bfloat16):
    return jnp.clip(scale * jax.random.normal(key, dims, jnp.float32), -most, most).astype(kind)


def setup_inputs(seed: int = 0) -> dict:
    streams_of = jax.random.split(jax.random.key(seed), 3)
    field = draw_field(jax.random.fold_in(streams_of[2], 71), 0)
    start_basis = scatter_about(streams_of[1], (NY, RANK), 1.0, 6.0, jnp.float32)
    return {"field": field, "start_basis": start_basis}


def add_plane(total, plane):
    return (total + jnp.einsum('ysz,wsz->yw', plane, plane, precision=lax.Precision.HIGHEST), None)

def reference(field, start_basis):
    gram, unused = lax.scan(add_plane, jnp.zeros((NY, NY), jnp.float32), field)
    lower = jnp.linalg.cholesky(gram)
    factor_out = lower / jnp.sqrt(jnp.float32(NX * NS * NZ))
    basis = start_basis
    for step in range(ITERS):
        inner = jnp.dot(lower.T, basis, precision=lax.Precision.HIGHEST)
        wide = jnp.dot(lower, inner, precision=lax.Precision.HIGHEST)
        chol = jnp.linalg.cholesky(jnp.dot(wide.T, wide, precision=lax.Precision.HIGHEST))
        basis = jax.scipy.linalg.solve_triangular(chol, wide.T, lower=True).T
    core = jnp.einsum('yr,xysz->xrsz', basis, field, precision=lax.Precision.HIGHEST)
    return (factor_out, core)
```

```python
import functools

import jax
import jax.numpy as jnp
from jax import lax
from jax.experimental import pallas as pl
from jax.experimental.pallas import tpu as pltpu
from jax.sharding import PartitionSpec as P

ITERS = 2
B = 128
PANEL = 16
EXTRA = 0
MESH = pl.DeviceIdType.MESH
VMEM = pl.BlockSpec(memory_space=pltpu.VMEM)
HBM = pl.BlockSpec(memory_space=pltpu.HBM)
F32 = jnp.float32
BF16 = jnp.bfloat16


def pieces(a):
    hi = a.astype(BF16)
    return hi, (a - hi.astype(F32)).astype(BF16)


def dotp(a, b, ca, cb):
    (ah, al), (bh, bl) = a, b
    return lax.dot_general(
        jnp.concatenate([ah, ah, al], axis=ca),
        jnp.concatenate([bh, bl, bh], axis=cb),
        (((ca,), (cb,)), ((), ())),
        preferred_element_type=F32,
    )


def dot3(a, b, ca, cb):
    return dotp(pieces(a), pieces(b), ca, cb)


def above(nb):
    return [(i, j) for i in range(nb) for j in range(i + 1, nb)]


def upper(nb):
    return [(i, j) for i in range(nb) for j in range(i, nb)]


def halvings(lo, hi):
    if hi - lo < 2:
        return []
    mid = (lo + hi) // 2
    return [(lo, mid, hi)] + halvings(lo, mid) + halvings(mid, hi)


def factor_blocks(refs, between=()):
    between = list(between)
    panels = B // PANEL
    sub = lax.broadcasted_iota(jnp.int32, (PANEL, B), 0)
    for p, lo in enumerate(range(0, B, PANEL)):
        for ref in refs:
            a = ref[lo:lo + PANEL, :B]
            e = ref[lo:lo + PANEL, B:]
            cols = [jnp.broadcast_to(a[:, lo + k:lo + k + 1], (PANEL, B)) for k in range(PANEL)]
            for j in range(PANEL):
                r = lax.rsqrt(cols[j][j:j + 1])
                coef = jnp.where(sub > j, cols[j] * r, 0.0)
                ua, ue = a[j:j + 1] * r, e[j:j + 1] * r
                a = jnp.where(sub == j, ua, a - coef * ua)
                e = jnp.where(sub == j, ue, e - coef * ue)
                for k in range(j + 1, PANEL):
                    cols[k] = cols[k] - coef * (cols[k][j:j + 1] * r)
            ref[lo:lo + PANEL, :B] = a
            ref[lo:lo + PANEL, B:] = e
            if lo + PANEL < B:
                u = jnp.concatenate([a, e], axis=1)
                ah = a.astype(BF16).astype(F32)
                al = a - ah
                uh = u.astype(BF16).astype(F32)
                ul = u - uh
                lhs = jnp.concatenate([ah, ah, al, al], axis=0).astype(BF16)
                rhs = jnp.concatenate([uh, ul, uh, ul], axis=0).astype(BF16)
                down = lax.dot_general(
                    lhs, rhs, (((0,), (0,)), ((), ())), preferred_element_type=F32
                )
                ref[lo + PANEL:, :] -= down[lo + PANEL:]
        share = -(-len(between) // (panels - p))
        for step in between[:share]:
            step()
        between = between[share:]


def load_block(step, r, m_g, eye):
    lo, hi = step * B, (step + 1) * B
    m_g[:, :B] = r[lo:hi, lo:hi]
    m_g[:, B:] = eye


def finish_block(step, r, m_g, row, col):
    lo, hi = step * B, (step + 1) * B
    r[lo:hi, lo:hi] = jnp.where(row <= col, m_g[:, :B], 0.0)
    if hi < r.shape[0]:
        u = dot3(jnp.where(row >= col, m_g[:, B:], 0.0), r[lo:hi, hi:], 1, 0)
        r[lo:hi, hi:] = u
        r[hi:, hi:] -= dot3(u, u, 0, 0)


def kernel(
    sizes, columns, field, start, core, factor, reg, xreg, fcat, own, sbuf, basis_t,
    part, tmp_c, tmp_g, tmp_y, full, diag, part_d, tmp_dc, tmp_dg, full_d,
    gh, gl, r, m_g, m_s, proj,
    sems, ssem, rsem, lsem, xssem, xrsem, xlsem, osem, bsem, cssem, crsem,
):
    n_gx, n_gy, n_gz = sizes
    gx, gy, gz = (lax.axis_index(a) for a in ("gx", "gy", "gz"))
    planes, rows, species = field.shape[0], field.shape[1], field.shape[2]
    quarter = species // n_gy
    chunks = planes * quarter
    extra = EXTRA
    n = reg.shape[1]
    nb = n // B
    kept = B // n_gy
    width = reg.shape[2]

    def peer(axis, index):
        where = {"gx": gx, "gy": gy, "gz": gz}
        where[axis] = index
        return (where["gx"], where["gy"], where["gz"])

    half_y = n_gy // 2

    def mirror(d):
        return lax.rem(d + half_y, n_gy)

    first_near = lax.div(gy, half_y) * half_y
    near = [first_near + lax.rem(gy - first_near + k, half_y) for k in range(1, half_y)]
    side = lax.rem(gz, 2)
    partner = peer("gz", gz + 1 - 2 * side)
    half = lax.div(gz, 2)
    y_peers = [lax.rem(gy + k, n_gy) for k in range(1, n_gy)]
    offsets = [(dx, dg) for dx in range(2) for dg in range(n_gx) if dx or dg]
    plane = []
    for dx, dg in offsets:
        h, g = lax.rem(half + dx, 2), lax.rem(gx + dg, n_gx)
        plane.append((h, g, (g, gy, 2 * h + side)))
    came_from = []
    for dx, dg in offsets:
        came_from.append((lax.rem(half + 2 - dx, 2), lax.rem(gx + n_gx - dg, n_gx)))
    greet = [peer("gy", d) for d in y_peers] + [who for _, _, who in plane] + [partner]
    barrier = pltpu.get_barrier_semaphore()
    for who in greet:
        pl.semaphore_signal(barrier, inc=1, device_id=who, device_id_type=MESH)
    pl.semaphore_wait(barrier, len(greet))

    mine = pl.ds(pl.multiple_of(gy * rows, rows), rows)

    def send(c, k):
        x, s = c // quarter, c % quarter
        d = y_peers[k]
        return pltpu.make_async_remote_copy(
            src_ref=field.at[x, :, d * quarter + s, :],
            dst_ref=reg.at[c, mine, :],
            send_sem=ssem.at[c, k],
            recv_sem=rsem.at[c, k],
            device_id=peer("gy", d),
            device_id_type=MESH,
        )

    def keep(c):
        x, s = c // quarter, c % quarter
        return pltpu.make_async_copy(
            field.at[x, :, gy * quarter + s, :], reg.at[c, mine, :], lsem.at[c]
        )

    @pl.loop(0, chunks)
    def _(c):
        for k in range(n_gy - 1):
            send(c, k).start()
        keep(c).start()

    def keep_own(q):
        return pltpu.make_async_copy(
            field.at[q // species, :, q % species, :], own.at[q], osem.at[q]
        )

    @pl.loop(0, own.shape[0])
    def _(q):
        keep_own(q).start()

    fetch = pltpu.make_async_copy(start, sbuf, bsem.at[0])
    fetch.start()

    def send_more(e, k):
        c = chunks - extra + e
        x, s = c // quarter, c % quarter
        d = y_peers[k]
        return pltpu.make_async_remote_copy(
            src_ref=field.at[x, :, mirror(d) * quarter + s, :],
            dst_ref=xreg.at[e, mine, :],
            send_sem=xssem.at[e, k],
            recv_sem=xrsem.at[e, k],
            device_id=peer("gy", d),
            device_id_type=MESH,
        )

    def keep_more(e):
        c = chunks - extra + e
        x, s = c // quarter, c % quarter
        return pltpu.make_async_copy(
            field.at[x, :, mirror(gy) * quarter + s, :], xreg.at[e, mine, :], xlsem.at[e]
        )

    def start_more(e):
        for k in range(n_gy - 1):
            send_more(e, k).start()
        keep_more(e).start()

    used = [0]

    def swap(src, dst, who):
        s = used[0]
        used[0] += 1
        cp = pltpu.make_async_remote_copy(
            src_ref=src, dst_ref=dst, send_sem=sems.at[0, s], recv_sem=sems.at[1, s],
            device_id=who, device_id_type=MESH,
        )
        cp.start()
        return cp

    def span(at, size):
        return pl.ds(pl.multiple_of(at, 8), size)

    row = lax.broadcasted_iota(jnp.int32, (B, B), 0)
    col = lax.broadcasted_iota(jnp.int32, (B, B), 1)
    eye = jnp.where(row == col, 1.0, 0.0).astype(F32)
    diag[...] = jnp.zeros_like(diag)

    @pl.loop(0, own.shape[0])
    def _(q):
        keep_own(q).wait()
        f = own[q]
        diag[...] += dot3(f, f, 1, 1)

    n_p = 2 * n_gx
    rows_d = part_d.shape[1]
    for p in range(2 * n_p):
        part_d[p] = diag[p * rows_d:(p + 1) * rows_d]
    cp = swap(part_d.at[pl.ds((1 - side) * n_p, n_p)], tmp_dc, partner)
    fetch.wait()
    basis_t[...] = sbuf[...].T
    part[...] = jnp.zeros_like(part)
    r[...] = jnp.zeros_like(r)
    cp.wait()
    for p in range(n_p):
        part_d[side * n_p + p] += tmp_dc[p]
    cps = []
    for k, (h, g, who) in enumerate(plane):
        cps.append(swap(part_d.at[side * n_p + h * n_gx + g], tmp_dg.at[k], who))

    blocks = above(nb)

    def gather(c):
        for k in range(n_gy - 1):
            send(c, k).wait()
        keep(c).wait()
        fh, fl = pieces(reg[c])
        fcat[c, :, :width] = fh
        fcat[c, :, width:] = fl
        for lo, mid, hi in halvings(0, nb):
            a, z = slice(lo * B, mid * B), slice(mid * B, hi * B)
            res = dotp((fh[a], fl[a]), (fh[z], fl[z]), 1, 1)
            for i in range(lo, mid):
                for j in range(mid, hi):
                    b = blocks.index((i, j))
                    part[b * B:(b + 1) * B, :] += res[
                        (i - lo) * B:(i - lo + 1) * B, (j - mid) * B:(j - mid + 1) * B
                    ]

    def gathers(lo, hi):
        @pl.loop(lo, hi)
        def _(c):
            gather(c)

    gathers(0, 1)
    for cp in cps:
        cp.wait()
    mine_d = side * n_p + half * n_gx + gx
    acc = part_d[mine_d]
    for k in range(len(plane)):
        acc += tmp_dg[k]
    full_d[gy, mine_d] = acc
    cps = []
    for d in y_peers:
        here = full_d.at[gy, mine_d]
        cps.append(swap(here, here, peer("gy", d)))
    gathers(1, 2)
    for cp in cps:
        cp.wait()
    here = full_d.at[:, mine_d]
    plane_d = [swap(here, here, who) for _, _, who in plane]
    onward = [swap(here, here, partner)]
    gathers(2, 3)
    for cp, (h, g) in zip(plane_d, came_from):
        cp.wait()
        here = full_d.at[:, side * n_p + h * n_gx + g]
        onward.append(swap(here, here, partner))
    gathers(3, 4)
    for cp in onward:
        cp.wait()
    for i in range(nb):
        for p in range(2 * n_p):
            there = slice(i * B + p * rows_d, i * B + (p + 1) * rows_d)
            block = full_d[i, p]
            r[there, i * B:(i + 1) * B] = block
    for i in range(nb):
        here = slice(i * B, (i + 1) * B)
        gh[here, here], gl[here, here] = pieces(r[here, here])
    load_block(0, r, m_g, eye)
    factor_blocks([m_g])
    gathers(4, chunks - 1)
    if extra:
        start_more(0)
    gathers(chunks - 1, chunks)

    total = part.shape[0]
    n_c = total // 2
    keep_c = side * n_c
    n_g = n_c // n_p
    cp = swap(part.at[span(n_c - keep_c, n_c), :], tmp_c, partner)
    cp.wait()
    part[span(keep_c, n_c), :] += tmp_c[...]

    def piece(h, g):
        return span(keep_c + (h * n_gx + g) * n_g, n_g)

    mine_g = piece(half, gx)
    cps = []
    for k, (h, g, who) in enumerate(plane):
        cps.append(swap(part.at[piece(h, g), :], tmp_g.at[k], who))
    for cp in cps:
        cp.wait()
    acc = part[mine_g, :]
    for k in range(len(plane)):
        acc += tmp_g[k]
    part[mine_g, :] = acc
    cps = []
    for k, d in enumerate(y_peers):
        cps.append(swap(part.at[mine_g, :], tmp_y.at[k], peer("gy", d)))
    for cp in cps:
        cp.wait()
    acc = part[mine_g, :]
    for k in range(n_gy - 1):
        acc += tmp_y[k]
    full[mine_g, :] = acc
    here = full.at[mine_g, :]
    plane_g = [swap(here, here, who) for _, _, who in plane]
    onward = [swap(here, here, partner)]
    for e in range(1, extra):
        start_more(e)
    for cp, (h, g) in zip(plane_g, came_from):
        cp.wait_recv()
        here = full.at[piece(h, g), :]
        onward.append(swap(here, here, partner))
    for cp in plane_g:
        cp.wait_send()
    for cp in onward:
        cp.wait()

    for b, (i, j) in enumerate(blocks):
        block = full[b * B:(b + 1) * B, :]
        there = (slice(i * B, (i + 1) * B), slice(j * B, (j + 1) * B))
        gh[there], gl[there] = pieces(block)
        gh[there[::-1]], gl[there[::-1]] = pieces(block.T)
        r[there] = block

    def apply_gram():
        return dotp(pieces(basis_t[...]), (gh[...], gl[...]), 1, 0)

    def load_small(wide):
        m_s[:, :B] = dotp(wide, wide, 1, 1)
        m_s[:, B:] = eye

    def small_inverse():
        return pieces(jnp.where(row >= col, m_s[:, B:], 0.0))

    for step in range(ITERS - 1):
        wide = pieces(apply_gram())
        load_small(wide)
        if step == 0:
            factor_blocks([m_s], [lambda: finish_block(0, r, m_g, row, col)])
            load_block(1, r, m_g, eye)
        else:
            factor_blocks([m_s])
        basis_t[...] = dotp(small_inverse(), wide, 1, 0)
    wide = pieces(apply_gram())
    load_small(wide)
    left = jnp.concatenate(wide, axis=0)

    def project(c):
        f = fcat[c]
        res = jnp.dot(left, f, preferred_element_type=F32)
        proj[c] = (res[B:, :width] + res[:B, width:]) + res[:B, :width]

    factor_blocks([m_s, m_g], [functools.partial(project, c) for c in range(chunks)])
    for e in range(extra):
        for k in range(n_gy - 1):
            send_more(e, k).wait()
        keep_more(e).wait()
        fh, fl = pieces(xreg[e])
        fcat[chunks + e, :, :width] = fh
        fcat[chunks + e, :, width:] = fl
        project(chunks + e)
    inverse = small_inverse()
    cps = []
    used_c = [0]

    def give(c, x, s, d):
        k = used_c[0]
        used_c[0] += 1
        cp = pltpu.make_async_remote_copy(
            src_ref=proj.at[c, span(d * kept, kept), :], dst_ref=core.at[x, s],
            send_sem=cssem.at[k], recv_sem=crsem.at[k],
            device_id=peer("gy", d), device_id_type=MESH,
        )
        cp.start()
        cps.append(cp)

    for c in range(chunks + extra):
        own_c = c if c < chunks else c - extra
        x, s = own_c // quarter, own_c % quarter
        s = s + (gy if c < chunks else mirror(gy)) * quarter
        proj[c] = dotp(inverse, pieces(proj[c]), 1, 0)
        for d in (y_peers if c < chunks - extra else near):
            give(c, x, s, d)
        core[x, s] = proj[c, span(gy * kept, kept), :]

    for step in range(1, nb):
        if step > 1:
            load_block(step, r, m_g, eye)
            factor_blocks([m_g])
        finish_block(step, r, m_g, row, col)
    scale = 1.0 / jnp.sqrt(F32(columns))
    factor[...] = jnp.zeros_like(factor)
    for i, j in upper(nb):
        @pl.when((gy == j) & (gz == i))
        def _():
            factor[...] = r[i * B:(i + 1) * B, j * B:(j + 1) * B].T * scale
    for cp in cps:
        cp.wait()


def per_device(sizes, field, start_basis):
    n_gx, n_gy, n_gz = sizes
    planes, rows, species, width = field.shape
    n, rank = start_basis.shape
    quarter = species // n_gy
    chunks = planes * quarter
    nb = n // B
    total = len(above(nb)) * B
    columns = planes * n_gx * species * width * n_gz
    n_g = total // 4 // n_gx
    others = 2 * n_gx - 1
    n_sems = 2 * (1 + others + (n_gy - 1) + 2 * others + 1)
    rows_d = B // (4 * n_gx)
    held = max(EXTRA, 1)
    n_give = (chunks - EXTRA) * (n_gy - 1) + 2 * EXTRA * (n_gy // 2 - 1)
    dma = pltpu.SemaphoreType.DMA
    core, factor = pl.pallas_call(
        functools.partial(kernel, sizes, columns),
        out_shape=(
            jax.ShapeDtypeStruct((planes, species, rank // n_gy, width), F32),
            jax.ShapeDtypeStruct((n // n_gy, n // n_gz), F32),
        ),
        in_specs=[HBM, HBM],
        out_specs=(VMEM, VMEM),
        scratch_shapes=[
            pltpu.VMEM((chunks, n, width), F32),
            pltpu.VMEM((held, n, width), F32),
            pltpu.VMEM((chunks + EXTRA, n, 2 * width), BF16),
            pltpu.VMEM((planes * species, rows, width), F32),
            pltpu.VMEM((n, rank), F32),
            pltpu.VMEM((rank, n), F32),
            pltpu.VMEM((total, B), F32),
            pltpu.VMEM((total // 2, B), F32),
            pltpu.VMEM((others, n_g, B), F32),
            pltpu.VMEM((n_gy - 1, n_g, B), F32),
            pltpu.VMEM((total, B), F32),
            pltpu.VMEM((B, B), F32),
            pltpu.VMEM((4 * n_gx, rows_d, B), F32),
            pltpu.VMEM((2 * n_gx, rows_d, B), F32),
            pltpu.VMEM((others, rows_d, B), F32),
            pltpu.VMEM((n_gy, 4 * n_gx, rows_d, B), F32),
            pltpu.VMEM((n, n), BF16),
            pltpu.VMEM((n, n), BF16),
            pltpu.VMEM((n, n), F32),
            pltpu.VMEM((B, 2 * B), F32),
            pltpu.VMEM((B, 2 * B), F32),
            pltpu.VMEM((chunks + EXTRA, rank, width), F32),
            dma((2, n_sems)),
            dma((chunks, n_gy - 1)),
            dma((chunks, n_gy - 1)),
            dma((chunks,)),
            dma((held, n_gy - 1)),
            dma((held, n_gy - 1)),
            dma((held,)),
            dma((planes * species,)),
            dma((1,)),
            dma((n_give,)),
            dma((n_give,)),
        ],
        compiler_params=pltpu.CompilerParams(
            collective_id=0, has_side_effects=True, vmem_limit_bytes=40 << 20
        ),
        name="step",
    )(field, start_basis)
    return factor, jnp.transpose(core, (0, 2, 1, 3))


def solution(mesh):
    sizes = tuple(mesh.shape[a] for a in ("gx", "gy", "gz"))
    return jax.shard_map(
        functools.partial(per_device, sizes),
        mesh=mesh,
        in_specs=(P("gx", "gy", None, "gz"), P()),
        out_specs=(P("gy", "gz"), P("gx", "gy", None, "gz")),
        check_vma=False,
    )
```

```python
import functools

import jax
import jax.numpy as jnp
from jax import lax
from jax.experimental import pallas as pl
from jax.experimental.pallas import tpu as pltpu
from jax.sharding import PartitionSpec as P

ITERS = 2
B = 128
PANEL = 16
EXTRA = 1
AHEAD = 3
MESH = pl.DeviceIdType.MESH
VMEM = pl.BlockSpec(memory_space=pltpu.VMEM)
HBM = pl.BlockSpec(memory_space=pltpu.HBM)
F32 = jnp.float32
BF16 = jnp.bfloat16


def pieces(a):
    hi = a.astype(BF16)
    return hi, (a - hi.astype(F32)).astype(BF16)


def dotp(a, b, ca, cb):
    (ah, al), (bh, bl) = a, b
    return lax.dot_general(
        jnp.concatenate([ah, ah, al], axis=ca),
        jnp.concatenate([bh, bl, bh], axis=cb),
        (((ca,), (cb,)), ((), ())),
        preferred_element_type=F32,
    )


def dot3(a, b, ca, cb):
    return dotp(pieces(a), pieces(b), ca, cb)


def above(nb):
    return [(i, j) for i in range(nb) for j in range(i + 1, nb)]


def upper(nb):
    return [(i, j) for i in range(nb) for j in range(i, nb)]


def halvings(lo, hi):
    if hi - lo < 2:
        return []
    mid = (lo + hi) // 2
    return [(lo, mid, hi)] + halvings(lo, mid) + halvings(mid, hi)


def factor_blocks(refs, between=()):
    between = list(between)
    panels = B // PANEL
    sub = lax.broadcasted_iota(jnp.int32, (PANEL, B), 0)
    for p, lo in enumerate(range(0, B, PANEL)):
        for ref in refs:
            a = ref[lo:lo + PANEL, :B]
            e = ref[lo:lo + PANEL, B:]
            cols = [jnp.broadcast_to(a[:, lo + k:lo + k + 1], (PANEL, B)) for k in range(PANEL)]
            for j in range(PANEL):
                r = lax.rsqrt(cols[j][j:j + 1])
                coef = jnp.where(sub > j, cols[j] * r, 0.0)
                ua, ue = a[j:j + 1] * r, e[j:j + 1] * r
                a = jnp.where(sub == j, ua, a - coef * ua)
                e = jnp.where(sub == j, ue, e - coef * ue)
                for k in range(j + 1, PANEL):
                    cols[k] = cols[k] - coef * (cols[k][j:j + 1] * r)
            ref[lo:lo + PANEL, :B] = a
            ref[lo:lo + PANEL, B:] = e
            if lo + PANEL < B:
                u = jnp.concatenate([a, e], axis=1)
                ah = a.astype(BF16).astype(F32)
                al = a - ah
                uh = u.astype(BF16).astype(F32)
                ul = u - uh
                lhs = jnp.concatenate([ah, ah, al, al], axis=0).astype(BF16)
                rhs = jnp.concatenate([uh, ul, uh, ul], axis=0).astype(BF16)
                down = lax.dot_general(
                    lhs, rhs, (((0,), (0,)), ((), ())), preferred_element_type=F32
                )
                ref[lo + PANEL:, :] -= down[lo + PANEL:]
        share = -(-len(between) // (panels - p))
        for step in between[:share]:
            step()
        between = between[share:]


def load_block(step, r, m_g, eye):
    lo, hi = step * B, (step + 1) * B
    m_g[:, :B] = r[lo:hi, lo:hi]
    m_g[:, B:] = eye


def finish_block(step, r, m_g, row, col):
    lo, hi = step * B, (step + 1) * B
    r[lo:hi, lo:hi] = jnp.where(row <= col, m_g[:, :B], 0.0)
    if hi < r.shape[0]:
        u = dot3(jnp.where(row >= col, m_g[:, B:], 0.0), r[lo:hi, hi:], 1, 0)
        r[lo:hi, hi:] = u
        r[hi:, hi:] -= dot3(u, u, 0, 0)


def kernel(
    sizes, columns, field, start, core, factor, reg, xreg, fcat, own, sbuf, basis_t,
    part, tmp_c, tmp_g, tmp_y, full, diag, part_d, tmp_dc, tmp_dg, full_d,
    gh, gl, r, m_g, m_s, proj,
    sems, ssem, rsem, lsem, xssem, xrsem, xlsem, osem, bsem, cssem, crsem, clsem,
):
    n_gx, n_gy, n_gz = sizes
    gx, gy, gz = (lax.axis_index(a) for a in ("gx", "gy", "gz"))
    planes, rows, species = field.shape[0], field.shape[1], field.shape[2]
    quarter = species // n_gy
    chunks = planes * quarter
    extra = EXTRA
    n = reg.shape[1]
    nb = n // B
    kept = B // n_gy
    width = reg.shape[2]

    def peer(axis, index):
        where = {"gx": gx, "gy": gy, "gz": gz}
        where[axis] = index
        return (where["gx"], where["gy"], where["gz"])

    half_y = n_gy // 2

    def mirror(d):
        return lax.rem(d + half_y, n_gy)

    first_near = lax.div(gy, half_y) * half_y
    near = [first_near + lax.rem(gy - first_near + k, half_y) for k in range(1, half_y)]
    side = lax.rem(gz, 2)
    partner = peer("gz", gz + 1 - 2 * side)
    half = lax.div(gz, 2)
    y_peers = [lax.rem(gy + k, n_gy) for k in range(1, n_gy)]
    offsets = [(dx, dg) for dx in range(2) for dg in range(n_gx) if dx or dg]
    plane = []
    for dx, dg in offsets:
        h, g = lax.rem(half + dx, 2), lax.rem(gx + dg, n_gx)
        plane.append((h, g, (g, gy, 2 * h + side)))
    came_from = []
    for dx, dg in offsets:
        came_from.append((lax.rem(half + 2 - dx, 2), lax.rem(gx + n_gx - dg, n_gx)))
    greet = [peer("gy", d) for d in y_peers] + [who for _, _, who in plane] + [partner]
    barrier = pltpu.get_barrier_semaphore()
    for who in greet:
        pl.semaphore_signal(barrier, inc=1, device_id=who, device_id_type=MESH)
    pl.semaphore_wait(barrier, len(greet))

    mine = pl.ds(pl.multiple_of(gy * rows, rows), rows)

    def send(c, k):
        x, s = c // quarter, c % quarter
        d = y_peers[k]
        return pltpu.make_async_remote_copy(
            src_ref=field.at[x, :, d * quarter + s, :],
            dst_ref=reg.at[c, mine, :],
            send_sem=ssem.at[c, k],
            recv_sem=rsem.at[c, k],
            device_id=peer("gy", d),
            device_id_type=MESH,
        )

    def keep(c):
        x, s = c // quarter, c % quarter
        return pltpu.make_async_copy(
            field.at[x, :, gy * quarter + s, :], reg.at[c, mine, :], lsem.at[c]
        )

    def post(c):
        for k in range(n_gy - 1):
            send(c, k).start()

    for c in range(AHEAD):
        post(c)

    def keep_own(q):
        return pltpu.make_async_copy(
            field.at[q // species, :, q % species, :], own.at[q], osem.at[q]
        )

    @pl.loop(0, own.shape[0])
    def _(q):
        keep_own(q).start()

    @pl.loop(0, chunks)
    def _(c):
        keep(c).start()

    fetch = pltpu.make_async_copy(start, sbuf, bsem.at[0])
    fetch.start()

    def send_more(e, k):
        c = chunks - extra + e
        x, s = c // quarter, c % quarter
        d = y_peers[k]
        return pltpu.make_async_remote_copy(
            src_ref=field.at[x, :, mirror(d) * quarter + s, :],
            dst_ref=xreg.at[e, mine, :],
            send_sem=xssem.at[e, k],
            recv_sem=xrsem.at[e, k],
            device_id=peer("gy", d),
            device_id_type=MESH,
        )

    def keep_more(e):
        c = chunks - extra + e
        x, s = c // quarter, c % quarter
        return pltpu.make_async_copy(
            field.at[x, :, mirror(gy) * quarter + s, :], xreg.at[e, mine, :], xlsem.at[e]
        )

    def start_more(e):
        for k in range(n_gy - 1):
            send_more(e, k).start()
        keep_more(e).start()

    used = [0]

    def swap(src, dst, who):
        s = used[0]
        used[0] += 1
        cp = pltpu.make_async_remote_copy(
            src_ref=src, dst_ref=dst, send_sem=sems.at[0, s], recv_sem=sems.at[1, s],
            device_id=who, device_id_type=MESH,
        )
        cp.start()
        return cp

    def span(at, size):
        return pl.ds(pl.multiple_of(at, 8), size)

    row = lax.broadcasted_iota(jnp.int32, (B, B), 0)
    col = lax.broadcasted_iota(jnp.int32, (B, B), 1)
    eye = jnp.where(row == col, 1.0, 0.0).astype(F32)
    diag[...] = jnp.zeros_like(diag)

    @pl.loop(0, own.shape[0])
    def _(q):
        keep_own(q).wait()
        f = own[q]
        diag[...] += dot3(f, f, 1, 1)

    n_p = 2 * n_gx
    rows_d = part_d.shape[1]
    for p in range(2 * n_p):
        part_d[p] = diag[p * rows_d:(p + 1) * rows_d]
    cp = swap(part_d.at[pl.ds((1 - side) * n_p, n_p)], tmp_dc, partner)
    fetch.wait()
    basis_t[...] = sbuf[...].T
    part[...] = jnp.zeros_like(part)
    r[...] = jnp.zeros_like(r)
    cp.wait()
    for p in range(n_p):
        part_d[side * n_p + p] += tmp_dc[p]
    cps = []
    for k, (h, g, who) in enumerate(plane):
        cps.append(swap(part_d.at[side * n_p + h * n_gx + g], tmp_dg.at[k], who))

    blocks = above(nb)

    def gather(c, more):
        for k in range(n_gy - 1):
            send(c, k).wait()
        if more:
            post(c + AHEAD)
        keep(c).wait()
        fh, fl = pieces(reg[c])
        fcat[c, :, :width] = fh
        fcat[c, :, width:] = fl
        for lo, mid, hi in halvings(0, nb):
            a, z = slice(lo * B, mid * B), slice(mid * B, hi * B)
            res = dotp((fh[a], fl[a]), (fh[z], fl[z]), 1, 1)
            for i in range(lo, mid):
                for j in range(mid, hi):
                    b = blocks.index((i, j))
                    part[b * B:(b + 1) * B, :] += res[
                        (i - lo) * B:(i - lo + 1) * B, (j - mid) * B:(j - mid + 1) * B
                    ]

    def gathers(lo, hi):
        @pl.loop(lo, min(hi, chunks - AHEAD))
        def _(c):
            gather(c, True)

        @pl.loop(max(lo, chunks - AHEAD), hi)
        def _(c):
            gather(c, False)

    gathers(0, 1)
    for cp in cps:
        cp.wait()
    mine_d = side * n_p + half * n_gx + gx
    acc = part_d[mine_d]
    for k in range(len(plane)):
        acc += tmp_dg[k]
    full_d[gy, mine_d] = acc
    cps = []
    for d in y_peers:
        here = full_d.at[gy, mine_d]
        cps.append(swap(here, here, peer("gy", d)))
    gathers(1, 4)
    for cp in cps:
        cp.wait()
    here = full_d.at[:, mine_d]
    plane_d = [swap(here, here, who) for _, _, who in plane]
    onward = [swap(here, here, partner)]
    gathers(4, 5)
    for cp, (h, g) in zip(plane_d, came_from):
        cp.wait()
        here = full_d.at[:, side * n_p + h * n_gx + g]
        onward.append(swap(here, here, partner))
    gathers(5, 6)
    for cp in onward:
        cp.wait()
    for i in range(nb):
        for p in range(2 * n_p):
            there = slice(i * B + p * rows_d, i * B + (p + 1) * rows_d)
            block = full_d[i, p]
            r[there, i * B:(i + 1) * B] = block
    for i in range(nb):
        here = slice(i * B, (i + 1) * B)
        gh[here, here], gl[here, here] = pieces(r[here, here])
    load_block(0, r, m_g, eye)
    factor_blocks([m_g])
    gathers(6, chunks - 1)
    gathers(chunks - 1, chunks)

    total = part.shape[0]
    n_c = total // 2
    keep_c = side * n_c
    n_g = n_c // n_p
    cp = swap(part.at[span(n_c - keep_c, n_c), :], tmp_c, partner)
    cp.wait()
    part[span(keep_c, n_c), :] += tmp_c[...]

    def piece(h, g):
        return span(keep_c + (h * n_gx + g) * n_g, n_g)

    mine_g = piece(half, gx)
    cps = []
    for k, (h, g, who) in enumerate(plane):
        cps.append(swap(part.at[piece(h, g), :], tmp_g.at[k], who))
    for cp in cps:
        cp.wait()
    acc = part[mine_g, :]
    for k in range(len(plane)):
        acc += tmp_g[k]
    part[mine_g, :] = acc
    cps = []
    for k, d in enumerate(y_peers):
        cps.append(swap(part.at[mine_g, :], tmp_y.at[k], peer("gy", d)))
    for cp in cps:
        cp.wait()
    acc = part[mine_g, :]
    for k in range(n_gy - 1):
        acc += tmp_y[k]
    full[mine_g, :] = acc
    here = full.at[mine_g, :]
    plane_g = [swap(here, here, who) for _, _, who in plane]
    onward = [swap(here, here, partner)]
    for e in range(extra):
        start_more(e)
    for cp, (h, g) in zip(plane_g, came_from):
        cp.wait_recv()
        here = full.at[piece(h, g), :]
        onward.append(swap(here, here, partner))
    for cp in plane_g:
        cp.wait_send()
    for cp in onward:
        cp.wait()

    for b, (i, j) in enumerate(blocks):
        block = full[b * B:(b + 1) * B, :]
        there = (slice(i * B, (i + 1) * B), slice(j * B, (j + 1) * B))
        gh[there], gl[there] = pieces(block)
        gh[there[::-1]], gl[there[::-1]] = pieces(block.T)
        r[there] = block

    def apply_gram():
        return dotp(pieces(basis_t[...]), (gh[...], gl[...]), 1, 0)

    def load_small(wide):
        m_s[:, :B] = dotp(wide, wide, 1, 1)
        m_s[:, B:] = eye

    def small_inverse():
        return pieces(jnp.where(row >= col, m_s[:, B:], 0.0))

    for step in range(ITERS - 1):
        wide = pieces(apply_gram())
        load_small(wide)
        factor_blocks([m_s], [lambda: finish_block(0, r, m_g, row, col)] if step == 0 else [])
        basis_t[...] = dotp(small_inverse(), wide, 1, 0)
    wide = pieces(apply_gram())
    load_small(wide)
    left = jnp.concatenate(wide, axis=0)

    def project(c):
        f = fcat[c]
        res = jnp.dot(left, f, preferred_element_type=F32)
        proj[c] = (res[B:, :width] + res[:B, width:]) + res[:B, :width]

    factor_blocks([m_s], [functools.partial(project, c) for c in range(chunks)])
    inverse = small_inverse()
    cps = []
    used_c = [0]

    def give(c, x, s, d):
        k = used_c[0]
        used_c[0] += 1
        cp = pltpu.make_async_remote_copy(
            src_ref=proj.at[c, span(d * kept, kept), :], dst_ref=core.at[x, :, s, :],
            send_sem=cssem.at[k], recv_sem=crsem.at[k],
            device_id=peer("gy", d), device_id_type=MESH,
        )
        cp.start()
        cps.append(cp)

    for c in range(chunks + extra):
        if c >= chunks:
            e = c - chunks
            for k in range(n_gy - 1):
                send_more(e, k).wait()
            keep_more(e).wait()
            fh, fl = pieces(xreg[e])
            fcat[c, :, :width] = fh
            fcat[c, :, width:] = fl
            project(c)
        own_c = c if c < chunks else c - extra
        x, s = own_c // quarter, own_c % quarter
        s = s + (gy if c < chunks else mirror(gy)) * quarter
        proj[c] = dotp(inverse, pieces(proj[c]), 1, 0)
        for d in (y_peers if c < chunks - extra else near):
            give(c, x, s, d)
        cp = pltpu.make_async_copy(
            proj.at[c, span(gy * kept, kept), :], core.at[x, :, s, :], clsem.at[c]
        )
        cp.start()
        cps.append(cp)

    for step in range(1, nb):
        load_block(step, r, m_g, eye)
        factor_blocks([m_g])
        finish_block(step, r, m_g, row, col)
    scale = 1.0 / jnp.sqrt(F32(columns))
    factor[...] = jnp.zeros_like(factor)
    for i, j in upper(nb):
        @pl.when((gy == j) & (gz == i))
        def _():
            factor[...] = r[i * B:(i + 1) * B, j * B:(j + 1) * B].T * scale
    for cp in cps:
        cp.wait()


def hand_over(core, factor, core_out, factor_out, sems):
    cps = [
        pltpu.make_async_copy(core, core_out, sems.at[0]),
        pltpu.make_async_copy(factor, factor_out, sems.at[1]),
    ]
    for cp in cps:
        cp.start()
    for cp in cps:
        cp.wait()


def per_device(sizes, field, start_basis):
    n_gx, n_gy, n_gz = sizes
    planes, rows, species, width = field.shape
    n, rank = start_basis.shape
    quarter = species // n_gy
    chunks = planes * quarter
    nb = n // B
    total = len(above(nb)) * B
    columns = planes * n_gx * species * width * n_gz
    n_g = total // 4 // n_gx
    others = 2 * n_gx - 1
    n_sems = 2 * (1 + others + (n_gy - 1) + 2 * others + 1)
    rows_d = B // (4 * n_gx)
    held = max(EXTRA, 1)
    n_give = (chunks - EXTRA) * (n_gy - 1) + 2 * EXTRA * (n_gy // 2 - 1)
    dma = pltpu.SemaphoreType.DMA
    outs = (
        jax.ShapeDtypeStruct((planes, rank // n_gy, species, width), F32),
        jax.ShapeDtypeStruct((n // n_gy, n // n_gz), F32),
    )
    core, factor = pl.pallas_call(
        functools.partial(kernel, sizes, columns),
        out_shape=outs,
        in_specs=[HBM, HBM],
        out_specs=(VMEM, VMEM),
        scratch_shapes=[
            pltpu.VMEM((chunks, n, width), F32),
            pltpu.VMEM((held, n, width), F32),
            pltpu.VMEM((chunks + EXTRA, n, 2 * width), BF16),
            pltpu.VMEM((planes * species, rows, width), F32),
            pltpu.VMEM((n, rank), F32),
            pltpu.VMEM((rank, n), F32),
            pltpu.VMEM((total, B), F32),
            pltpu.VMEM((total // 2, B), F32),
            pltpu.VMEM((others, n_g, B), F32),
            pltpu.VMEM((n_gy - 1, n_g, B), F32),
            pltpu.VMEM((total, B), F32),
            pltpu.VMEM((B, B), F32),
            pltpu.VMEM((4 * n_gx, rows_d, B), F32),
            pltpu.VMEM((2 * n_gx, rows_d, B), F32),
            pltpu.VMEM((others, rows_d, B), F32),
            pltpu.VMEM((n_gy, 4 * n_gx, rows_d, B), F32),
            pltpu.VMEM((n, n), BF16),
            pltpu.VMEM((n, n), BF16),
            pltpu.VMEM((n, n), F32),
            pltpu.VMEM((B, 2 * B), F32),
            pltpu.VMEM((B, 2 * B), F32),
            pltpu.VMEM((chunks + EXTRA, rank, width), F32),
            dma((2, n_sems)),
            dma((chunks, n_gy - 1)),
            dma((chunks, n_gy - 1)),
            dma((chunks,)),
            dma((held, n_gy - 1)),
            dma((held, n_gy - 1)),
            dma((held,)),
            dma((planes * species,)),
            dma((1,)),
            dma((n_give,)),
            dma((n_give,)),
            dma((chunks + EXTRA,)),
        ],
        compiler_params=pltpu.CompilerParams(
            collective_id=0, has_side_effects=True, vmem_limit_bytes=53 << 20
        ),
        name="step",
    )(field, start_basis)
    core, factor = pl.pallas_call(
        hand_over,
        out_shape=outs,
        in_specs=[VMEM, VMEM],
        out_specs=(HBM, HBM),
        scratch_shapes=[dma((2,))],
        compiler_params=pltpu.CompilerParams(vmem_limit_bytes=32 << 20),
        name="out",
    )(core, factor)
    return factor, core


def solution(mesh):
    sizes = tuple(mesh.shape[a] for a in ("gx", "gy", "gz"))
    return jax.shard_map(
        functools.partial(per_device, sizes),
        mesh=mesh,
        in_specs=(P("gx", "gy", None, "gz"), P()),
        out_specs=(P("gy", "gz"), P("gx", "gy", None, "gz")),
        check_vma=False,
    )
```

```python
import functools

import jax
import jax.numpy as jnp
from jax import lax
from jax.experimental import pallas as pl
from jax.experimental.pallas import tpu as pltpu
from jax.sharding import PartitionSpec as P

ITERS = 2
B = 128
PANEL = 16
EXTRA = 1
AHEAD = 3
PARTS = 3
MESH = pl.DeviceIdType.MESH
VMEM = pl.BlockSpec(memory_space=pltpu.VMEM)
HBM = pl.BlockSpec(memory_space=pltpu.HBM)
F32 = jnp.float32
BF16 = jnp.bfloat16


def pieces(a):
    hi = a.astype(BF16)
    return hi, (a - hi.astype(F32)).astype(BF16)


def dotp(a, b, ca, cb):
    (ah, al), (bh, bl) = a, b
    return lax.dot_general(
        jnp.concatenate([ah, ah, al], axis=ca),
        jnp.concatenate([bh, bl, bh], axis=cb),
        (((ca,), (cb,)), ((), ())),
        preferred_element_type=F32,
    )


def dot3(a, b, ca, cb):
    return dotp(pieces(a), pieces(b), ca, cb)


def above(nb):
    return [(i, j) for i in range(nb) for j in range(i + 1, nb)]


def upper(nb):
    return [(i, j) for i in range(nb) for j in range(i, nb)]


def halvings(lo, hi):
    if hi - lo < 2:
        return []
    mid = (lo + hi) // 2
    return [(lo, mid, hi)] + halvings(lo, mid) + halvings(mid, hi)


def factor_blocks(refs, between=()):
    between = list(between)
    panels = B // PANEL
    sub = lax.broadcasted_iota(jnp.int32, (PANEL, B), 0)
    for p, lo in enumerate(range(0, B, PANEL)):
        for ref in refs:
            a = ref[lo:lo + PANEL, :B]
            e = ref[lo:lo + PANEL, B:]
            cols = [jnp.broadcast_to(a[:, lo + k:lo + k + 1], (PANEL, B)) for k in range(PANEL)]
            for j in range(PANEL):
                r = lax.rsqrt(cols[j][j:j + 1])
                coef = jnp.where(sub > j, cols[j] * r, 0.0)
                ua, ue = a[j:j + 1] * r, e[j:j + 1] * r
                a = jnp.where(sub == j, ua, a - coef * ua)
                e = jnp.where(sub == j, ue, e - coef * ue)
                for k in range(j + 1, PANEL):
                    cols[k] = cols[k] - coef * (cols[k][j:j + 1] * r)
            ref[lo:lo + PANEL, :B] = a
            ref[lo:lo + PANEL, B:] = e
            if lo + PANEL < B:
                u = jnp.concatenate([a, e], axis=1)
                ah = a.astype(BF16).astype(F32)
                al = a - ah
                uh = u.astype(BF16).astype(F32)
                ul = u - uh
                lhs = jnp.concatenate([ah, ah, al, al], axis=0).astype(BF16)
                rhs = jnp.concatenate([uh, ul, uh, ul], axis=0).astype(BF16)
                down = lax.dot_general(
                    lhs, rhs, (((0,), (0,)), ((), ())), preferred_element_type=F32
                )
                ref[lo + PANEL:, :] -= down[lo + PANEL:]
        share = -(-len(between) // (panels - p))
        for step in between[:share]:
            step()
        between = between[share:]


def load_block(step, r, m_g, eye):
    lo, hi = step * B, (step + 1) * B
    m_g[:, :B] = r[lo:hi, lo:hi]
    m_g[:, B:] = eye


def finish_block(step, r, m_g, row, col):
    lo, hi = step * B, (step + 1) * B
    r[lo:hi, lo:hi] = jnp.where(row <= col, m_g[:, :B], 0.0)
    if hi < r.shape[0]:
        u = dot3(jnp.where(row >= col, m_g[:, B:], 0.0), r[lo:hi, hi:], 1, 0)
        r[lo:hi, hi:] = u
        r[hi:, hi:] -= dot3(u, u, 0, 0)


def kernel(
    sizes, columns, field, start, *refs,
):
    n_core = field.shape[0]
    core = refs[:n_core]
    (
    factor, reg, xreg, fcat, own, sbuf, basis_t,
    part, tmp_c, tmp_g, tmp_y, full, diag, part_d, tmp_dc, tmp_dg, full_d,
    gh, gl, r, m_g, m_s, proj,
    sems, ssem, rsem, lsem, xssem, xrsem, xlsem, osem, bsem, cssem, crsem, clsem,
    ) = refs[n_core:]
    n_gx, n_gy, n_gz = sizes
    gx, gy, gz = (lax.axis_index(a) for a in ("gx", "gy", "gz"))
    planes, rows, species = field.shape[0], field.shape[1], field.shape[2]
    quarter = species // n_gy
    chunks = planes * quarter
    extra = EXTRA
    n = reg.shape[1]
    nb = n // B
    kept = B // n_gy
    width = reg.shape[2]

    def peer(axis, index):
        where = {"gx": gx, "gy": gy, "gz": gz}
        where[axis] = index
        return (where["gx"], where["gy"], where["gz"])

    half_y = n_gy // 2

    def mirror(d):
        return lax.rem(d + half_y, n_gy)

    first_near = lax.div(gy, half_y) * half_y
    near = [first_near + lax.rem(gy - first_near + k, half_y) for k in range(1, half_y)]
    side = lax.rem(gz, 2)
    partner = peer("gz", gz + 1 - 2 * side)
    half = lax.div(gz, 2)
    y_peers = [lax.rem(gy + k, n_gy) for k in range(1, n_gy)]
    offsets = [(dx, dg) for dx in range(2) for dg in range(n_gx) if dx or dg]
    plane = []
    for dx, dg in offsets:
        h, g = lax.rem(half + dx, 2), lax.rem(gx + dg, n_gx)
        plane.append((h, g, (g, gy, 2 * h + side)))
    came_from = []
    for dx, dg in offsets:
        came_from.append((lax.rem(half + 2 - dx, 2), lax.rem(gx + n_gx - dg, n_gx)))
    greet = [peer("gy", d) for d in y_peers] + [who for _, _, who in plane] + [partner]
    barrier = pltpu.get_barrier_semaphore()
    for who in greet:
        pl.semaphore_signal(barrier, inc=1, device_id=who, device_id_type=MESH)
    pl.semaphore_wait(barrier, len(greet))

    mine = pl.ds(pl.multiple_of(gy * rows, rows), rows)

    def send(c, k):
        x, s = c // quarter, c % quarter
        d = y_peers[k]
        return pltpu.make_async_remote_copy(
            src_ref=field.at[x, :, d * quarter + s, :],
            dst_ref=reg.at[c, mine, :],
            send_sem=ssem.at[c, k],
            recv_sem=rsem.at[c, k],
            device_id=peer("gy", d),
            device_id_type=MESH,
        )

    def keep(c):
        x, s = c // quarter, c % quarter
        return pltpu.make_async_copy(
            field.at[x, :, gy * quarter + s, :], reg.at[c, mine, :], lsem.at[c]
        )

    def post(c):
        for k in range(n_gy - 1):
            send(c, k).start()

    for c in range(AHEAD):
        post(c)

    def keep_own(q):
        return pltpu.make_async_copy(
            field.at[q // species, :, q % species, :], own.at[q], osem.at[q]
        )

    @pl.loop(0, own.shape[0])
    def _(q):
        keep_own(q).start()

    @pl.loop(0, chunks)
    def _(c):
        keep(c).start()

    fetch = pltpu.make_async_copy(start, sbuf, bsem.at[0])
    fetch.start()

    def send_more(e, k):
        c = chunks - extra + e
        x, s = c // quarter, c % quarter
        d = y_peers[k]
        return pltpu.make_async_remote_copy(
            src_ref=field.at[x, :, mirror(d) * quarter + s, :],
            dst_ref=xreg.at[e, mine, :],
            send_sem=xssem.at[e, k],
            recv_sem=xrsem.at[e, k],
            device_id=peer("gy", d),
            device_id_type=MESH,
        )

    def keep_more(e):
        c = chunks - extra + e
        x, s = c // quarter, c % quarter
        return pltpu.make_async_copy(
            field.at[x, :, mirror(gy) * quarter + s, :], xreg.at[e, mine, :], xlsem.at[e]
        )

    def start_more(e):
        for k in range(n_gy - 1):
            send_more(e, k).start()
        keep_more(e).start()

    used = [0]

    def swap(src, dst, who):
        s = used[0]
        used[0] += 1
        cp = pltpu.make_async_remote_copy(
            src_ref=src, dst_ref=dst, send_sem=sems.at[0, s], recv_sem=sems.at[1, s],
            device_id=who, device_id_type=MESH,
        )
        cp.start()
        return cp

    def span(at, size):
        return pl.ds(pl.multiple_of(at, 8), size)

    row = lax.broadcasted_iota(jnp.int32, (B, B), 0)
    col = lax.broadcasted_iota(jnp.int32, (B, B), 1)
    eye = jnp.where(row == col, 1.0, 0.0).astype(F32)
    diag[...] = jnp.zeros_like(diag)

    @pl.loop(0, own.shape[0])
    def _(q):
        keep_own(q).wait()
        f = own[q]
        diag[...] += dot3(f, f, 1, 1)

    n_p = 2 * n_gx
    rows_d = part_d.shape[1]
    for p in range(2 * n_p):
        part_d[p] = diag[p * rows_d:(p + 1) * rows_d]
    cp = swap(part_d.at[pl.ds((1 - side) * n_p, n_p)], tmp_dc, partner)
    fetch.wait()
    basis_t[...] = sbuf[...].T
    part[...] = jnp.zeros_like(part)
    r[...] = jnp.zeros_like(r)
    cp.wait()
    for p in range(n_p):
        part_d[side * n_p + p] += tmp_dc[p]
    cps = []
    for k, (h, g, who) in enumerate(plane):
        cps.append(swap(part_d.at[side * n_p + h * n_gx + g], tmp_dg.at[k], who))

    blocks = above(nb)

    def gather(c, more):
        for k in range(n_gy - 1):
            send(c, k).wait()
        if more:
            post(c + AHEAD)
        keep(c).wait()
        fh, fl = pieces(reg[c])
        fcat[c, :, :width] = fh
        fcat[c, :, width:] = fl
        for lo, mid, hi in halvings(0, nb):
            a, z = slice(lo * B, mid * B), slice(mid * B, hi * B)
            res = dotp((fh[a], fl[a]), (fh[z], fl[z]), 1, 1)
            for i in range(lo, mid):
                for j in range(mid, hi):
                    b = blocks.index((i, j))
                    part[b * B:(b + 1) * B, :] += res[
                        (i - lo) * B:(i - lo + 1) * B, (j - mid) * B:(j - mid + 1) * B
                    ]

    def gathers(lo, hi):
        @pl.loop(lo, min(hi, chunks - AHEAD))
        def _(c):
            gather(c, True)

        @pl.loop(max(lo, chunks - AHEAD), hi)
        def _(c):
            gather(c, False)

    gathers(0, 1)
    for cp in cps:
        cp.wait()
    mine_d = side * n_p + half * n_gx + gx
    acc = part_d[mine_d]
    for k in range(len(plane)):
        acc += tmp_dg[k]
    full_d[gy, mine_d] = acc
    cps = []
    for d in y_peers:
        here = full_d.at[gy, mine_d]
        cps.append(swap(here, here, peer("gy", d)))
    gathers(1, 4)
    for cp in cps:
        cp.wait()
    here = full_d.at[:, mine_d]
    plane_d = [swap(here, here, who) for _, _, who in plane]
    onward = [swap(here, here, partner)]
    gathers(4, 5)
    for cp, (h, g) in zip(plane_d, came_from):
        cp.wait()
        here = full_d.at[:, side * n_p + h * n_gx + g]
        onward.append(swap(here, here, partner))
    gathers(5, 6)
    for cp in onward:
        cp.wait()
    for i in range(nb):
        for p in range(2 * n_p):
            there = slice(i * B + p * rows_d, i * B + (p + 1) * rows_d)
            block = full_d[i, p]
            r[there, i * B:(i + 1) * B] = block
    for i in range(nb):
        here = slice(i * B, (i + 1) * B)
        gh[here, here], gl[here, here] = pieces(r[here, here])
    load_block(0, r, m_g, eye)
    factor_blocks([m_g])
    gathers(6, chunks - 1)
    gathers(chunks - 1, chunks)

    total = part.shape[0]
    n_c = total // 2
    n_q = n_c // PARTS
    n_g = n_q // n_p
    keep_c = side * n_c

    def piece(q, h, g):
        return span(keep_c + q * n_q + (h * n_gx + g) * n_g, n_g)

    halves, planes_g, lines, spread = [], [], [], []
    for q in range(PARTS):
        there = span(n_c - keep_c + q * n_q, n_q)
        halves.append(swap(part.at[there, :], tmp_c.at[q], partner))
    for q in range(PARTS):
        halves[q].wait()
        part[span(keep_c + q * n_q, n_q), :] += tmp_c[q]
        planes_g.append([
            swap(part.at[piece(q, h, g), :], tmp_g.at[k, q], who)
            for k, (h, g, who) in enumerate(plane)
        ])
    for q in range(PARTS):
        for cp in planes_g[q]:
            cp.wait()
        mine_g = piece(q, half, gx)
        acc = part[mine_g, :]
        for k in range(len(plane)):
            acc += tmp_g[k, q]
        part[mine_g, :] = acc
        lines.append([
            swap(part.at[mine_g, :], tmp_y.at[k, q], peer("gy", d))
            for k, d in enumerate(y_peers)
        ])
    onward = []
    for q in range(PARTS):
        for cp in lines[q]:
            cp.wait()
        mine_g = piece(q, half, gx)
        acc = part[mine_g, :]
        for k in range(n_gy - 1):
            acc += tmp_y[k, q]
        full[mine_g, :] = acc
        here = full.at[mine_g, :]
        spread.append([swap(here, here, who) for _, _, who in plane])
        onward.append(swap(here, here, partner))
    for e in range(extra):
        start_more(e)
    for q in range(PARTS):
        for cp, (h, g) in zip(spread[q], came_from):
            cp.wait_recv()
            here = full.at[piece(q, h, g), :]
            onward.append(swap(here, here, partner))
    for cps in spread:
        for cp in cps:
            cp.wait_send()
    for cp in onward:
        cp.wait()

    for b, (i, j) in enumerate(blocks):
        block = full[b * B:(b + 1) * B, :]
        there = (slice(i * B, (i + 1) * B), slice(j * B, (j + 1) * B))
        gh[there], gl[there] = pieces(block)
        gh[there[::-1]], gl[there[::-1]] = pieces(block.T)
        r[there] = block

    def apply_gram():
        return dotp(pieces(basis_t[...]), (gh[...], gl[...]), 1, 0)

    def load_small(wide):
        m_s[:, :B] = dotp(wide, wide, 1, 1)
        m_s[:, B:] = eye

    def small_inverse():
        return pieces(jnp.where(row >= col, m_s[:, B:], 0.0))

    for step in range(ITERS - 1):
        wide = pieces(apply_gram())
        load_small(wide)
        factor_blocks([m_s], [lambda: finish_block(0, r, m_g, row, col)] if step == 0 else [])
        basis_t[...] = dotp(small_inverse(), wide, 1, 0)
    wide = pieces(apply_gram())
    load_small(wide)
    left = jnp.concatenate(wide, axis=0)

    def project(c):
        f = fcat[c]
        res = jnp.dot(left, f, preferred_element_type=F32)
        proj[c] = (res[B:, :width] + res[:B, width:]) + res[:B, :width]

    factor_blocks([m_s], [functools.partial(project, c) for c in range(chunks)])
    inverse = small_inverse()
    cps = []
    used_c = [0]

    def give(c, x, s, d):
        k = used_c[0]
        used_c[0] += 1
        cp = pltpu.make_async_remote_copy(
            src_ref=proj.at[c, span(d * kept, kept), :], dst_ref=core[x].at[:, s, :],
            send_sem=cssem.at[k], recv_sem=crsem.at[k],
            device_id=peer("gy", d), device_id_type=MESH,
        )
        cp.start()
        cps.append(cp)

    for c in range(chunks + extra):
        if c >= chunks:
            e = c - chunks
            for k in range(n_gy - 1):
                send_more(e, k).wait()
            keep_more(e).wait()
            fh, fl = pieces(xreg[e])
            fcat[c, :, :width] = fh
            fcat[c, :, width:] = fl
            project(c)
        own_c = c if c < chunks else c - extra
        x, s = own_c // quarter, own_c % quarter
        s = s + (gy if c < chunks else mirror(gy)) * quarter
        proj[c] = dotp(inverse, pieces(proj[c]), 1, 0)
        for d in (y_peers if c < chunks - extra else near):
            give(c, x, s, d)
        cp = pltpu.make_async_copy(
            proj.at[c, span(gy * kept, kept), :], core[x].at[:, s, :], clsem.at[c]
        )
        cp.start()
        cps.append(cp)

    for step in range(1, nb):
        load_block(step, r, m_g, eye)
        factor_blocks([m_g])
        finish_block(step, r, m_g, row, col)
    scale = 1.0 / jnp.sqrt(F32(columns))
    factor[...] = jnp.zeros_like(factor)
    for i, j in upper(nb):
        @pl.when((gy == j) & (gz == i))
        def _():
            factor[...] = r[i * B:(i + 1) * B, j * B:(j + 1) * B].T * scale
    for cp in cps:
        cp.wait()


def hand_over(*refs):
    *core, factor, core_out, factor_out, sems = refs
    cps = [pltpu.make_async_copy(c, core_out.at[x], sems.at[x]) for x, c in enumerate(core)]
    cps.append(pltpu.make_async_copy(factor, factor_out, sems.at[len(core)]))
    for cp in cps:
        cp.start()
    for cp in cps:
        cp.wait()


def per_device(sizes, field, start_basis):
    n_gx, n_gy, n_gz = sizes
    planes, rows, species, width = field.shape
    n, rank = start_basis.shape
    quarter = species // n_gy
    chunks = planes * quarter
    nb = n // B
    total = len(above(nb)) * B
    columns = planes * n_gx * species * width * n_gz
    n_g = total // 4 // n_gx // PARTS
    others = 2 * n_gx - 1
    n_sems = (1 + PARTS) * (1 + others + (n_gy - 1) + 2 * others + 1)
    rows_d = B // (4 * n_gx)
    held = max(EXTRA, 1)
    n_give = (chunks - EXTRA) * (n_gy - 1) + 2 * EXTRA * (n_gy // 2 - 1)
    dma = pltpu.SemaphoreType.DMA
    outs = (
        jax.ShapeDtypeStruct((planes, rank // n_gy, species, width), F32),
        jax.ShapeDtypeStruct((n // n_gy, n // n_gz), F32),
    )
    *cores, factor = pl.pallas_call(
        functools.partial(kernel, sizes, columns),
        out_shape=[jax.ShapeDtypeStruct(outs[0].shape[1:], F32)] * planes + [outs[1]],
        in_specs=[HBM, HBM],
        out_specs=[VMEM] * (planes + 1),
        scratch_shapes=[
            pltpu.VMEM((chunks, n, width), F32),
            pltpu.VMEM((held, n, width), F32),
            pltpu.VMEM((chunks + EXTRA, n, 2 * width), BF16),
            pltpu.VMEM((planes * species, rows, width), F32),
            pltpu.VMEM((n, rank), F32),
            pltpu.VMEM((rank, n), F32),
            pltpu.VMEM((total, B), F32),
            pltpu.VMEM((PARTS, total // 2 // PARTS, B), F32),
            pltpu.VMEM((others, PARTS, n_g, B), F32),
            pltpu.VMEM((n_gy - 1, PARTS, n_g, B), F32),
            pltpu.VMEM((total, B), F32),
            pltpu.VMEM((B, B), F32),
            pltpu.VMEM((4 * n_gx, rows_d, B), F32),
            pltpu.VMEM((2 * n_gx, rows_d, B), F32),
            pltpu.VMEM((others, rows_d, B), F32),
            pltpu.VMEM((n_gy, 4 * n_gx, rows_d, B), F32),
            pltpu.VMEM((n, n), BF16),
            pltpu.VMEM((n, n), BF16),
            pltpu.VMEM((n, n), F32),
            pltpu.VMEM((B, 2 * B), F32),
            pltpu.VMEM((B, 2 * B), F32),
            pltpu.VMEM((chunks + EXTRA, rank, width), F32),
            dma((2, n_sems)),
            dma((chunks, n_gy - 1)),
            dma((chunks, n_gy - 1)),
            dma((chunks,)),
            dma((held, n_gy - 1)),
            dma((held, n_gy - 1)),
            dma((held,)),
            dma((planes * species,)),
            dma((1,)),
            dma((n_give,)),
            dma((n_give,)),
            dma((chunks + EXTRA,)),
        ],
        compiler_params=pltpu.CompilerParams(
            collective_id=0, has_side_effects=True, vmem_limit_bytes=(53 << 20) + (320 << 10)
        ),
        name="step",
    )(field, start_basis)
    core, factor = pl.pallas_call(
        hand_over,
        out_shape=outs,
        in_specs=[VMEM] * (planes + 1),
        out_specs=(HBM, HBM),
        scratch_shapes=[dma((planes + 1,))],
        compiler_params=pltpu.CompilerParams(vmem_limit_bytes=32 << 20),
        name="out",
    )(*cores, factor)
    return factor, core


def solution(mesh):
    sizes = tuple(mesh.shape[a] for a in ("gx", "gy", "gz"))
    return jax.shard_map(
        functools.partial(per_device, sizes),
        mesh=mesh,
        in_specs=(P("gx", "gy", None, "gz"), P()),
        out_specs=(P("gy", "gz"), P("gx", "gy", None, "gz")),
        check_vma=False,
    )
```

```python
import functools

import jax
import jax.numpy as jnp
from jax import lax
from jax.experimental import pallas as pl
from jax.experimental.pallas import tpu as pltpu
from jax.sharding import PartitionSpec as P

ITERS = 2
B = 128
PANEL = 16
EXTRA = 1
AHEAD = 3
PARTS = 3
MESH = pl.DeviceIdType.MESH
VMEM = pl.BlockSpec(memory_space=pltpu.VMEM)
HBM = pl.BlockSpec(memory_space=pltpu.HBM)
F32 = jnp.float32
BF16 = jnp.bfloat16


def pieces(a):
    hi = a.astype(BF16)
    return hi, (a - hi.astype(F32)).astype(BF16)


def dotp(a, b, ca, cb):
    (ah, al), (bh, bl) = a, b
    return lax.dot_general(
        jnp.concatenate([ah, ah, al], axis=ca),
        jnp.concatenate([bh, bl, bh], axis=cb),
        (((ca,), (cb,)), ((), ())),
        preferred_element_type=F32,
    )


def dot3(a, b, ca, cb):
    return dotp(pieces(a), pieces(b), ca, cb)


def above(nb):
    return [(i, j) for i in range(nb) for j in range(i + 1, nb)]


def upper(nb):
    return [(i, j) for i in range(nb) for j in range(i, nb)]


def halvings(lo, hi):
    if hi - lo < 2:
        return []
    mid = (lo + hi) // 2
    return [(lo, mid, hi)] + halvings(lo, mid) + halvings(mid, hi)


def factor_blocks(refs, between=()):
    between = list(between)
    panels = B // PANEL
    sub = lax.broadcasted_iota(jnp.int32, (PANEL, B), 0)
    for p, lo in enumerate(range(0, B, PANEL)):
        for ref in refs:
            a = ref[lo:lo + PANEL, :B]
            e = ref[lo:lo + PANEL, B:]
            cols = [jnp.broadcast_to(a[:, lo + k:lo + k + 1], (PANEL, B)) for k in range(PANEL)]
            for j in range(PANEL):
                r = lax.rsqrt(cols[j][j:j + 1])
                coef = jnp.where(sub > j, cols[j] * r, 0.0)
                ua, ue = a[j:j + 1] * r, e[j:j + 1] * r
                a = jnp.where(sub == j, ua, a - coef * ua)
                e = jnp.where(sub == j, ue, e - coef * ue)
                for k in range(j + 1, PANEL):
                    cols[k] = cols[k] - coef * (cols[k][j:j + 1] * r)
            ref[lo:lo + PANEL, :B] = a
            ref[lo:lo + PANEL, B:] = e
            if lo + PANEL < B:
                u = jnp.concatenate([a, e], axis=1)
                ah = a.astype(BF16).astype(F32)
                al = a - ah
                uh = u.astype(BF16).astype(F32)
                ul = u - uh
                lhs = jnp.concatenate([ah, ah, al, al], axis=0).astype(BF16)
                rhs = jnp.concatenate([uh, ul, uh, ul], axis=0).astype(BF16)
                down = lax.dot_general(
                    lhs, rhs, (((0,), (0,)), ((), ())), preferred_element_type=F32
                )
                ref[lo + PANEL:, :] -= down[lo + PANEL:]
        share = -(-len(between) // (panels - p))
        for step in between[:share]:
            step()
        between = between[share:]


def load_block(step, r, m_g, eye):
    lo, hi = step * B, (step + 1) * B
    m_g[:, :B] = r[lo:hi, lo:hi]
    m_g[:, B:] = eye


def finish_block(step, r, m_g, row, col):
    lo, hi = step * B, (step + 1) * B
    r[lo:hi, lo:hi] = jnp.where(row <= col, m_g[:, :B], 0.0)
    if hi < r.shape[0]:
        u = dot3(jnp.where(row >= col, m_g[:, B:], 0.0), r[lo:hi, hi:], 1, 0)
        r[lo:hi, hi:] = u
        r[hi:, hi:] -= dot3(u, u, 0, 0)


def kernel(
    sizes, columns, field, start, *refs,
):
    n_core = field.shape[0]
    core = refs[:n_core]
    (
    factor, reg, xreg, fcat, own, sbuf, basis_t,
    part, tmp_c, tmp_g, tmp_y, full, diag, part_d, tmp_dc, tmp_dg, full_d,
    gh, gl, r, m_g, m_s, proj,
    sems, ssem, rsem, lsem, xssem, xrsem, xlsem, osem, bsem, cssem, crsem, clsem,
    ) = refs[n_core:]
    n_gx, n_gy, n_gz = sizes
    gx, gy, gz = (lax.axis_index(a) for a in ("gx", "gy", "gz"))
    planes, rows, species = field.shape[0], field.shape[1], field.shape[2]
    quarter = species // n_gy
    chunks = planes * quarter
    extra = EXTRA
    n = reg.shape[1]
    nb = n // B
    kept = B // n_gy
    width = reg.shape[2]

    def peer(axis, index):
        where = {"gx": gx, "gy": gy, "gz": gz}
        where[axis] = index
        return (where["gx"], where["gy"], where["gz"])

    half_y = n_gy // 2

    def mirror(d):
        return lax.rem(d + half_y, n_gy)

    first_near = lax.div(gy, half_y) * half_y
    near = [first_near + lax.rem(gy - first_near + k, half_y) for k in range(1, half_y)]
    side = lax.rem(gz, 2)
    partner = peer("gz", gz + 1 - 2 * side)
    half = lax.div(gz, 2)
    y_peers = [lax.rem(gy + k, n_gy) for k in range(1, n_gy)]
    offsets = [(dx, dg) for dx in range(2) for dg in range(n_gx) if dx or dg]
    plane = []
    for dx, dg in offsets:
        h, g = lax.rem(half + dx, 2), lax.rem(gx + dg, n_gx)
        plane.append((h, g, (g, gy, 2 * h + side)))
    came_from = []
    for dx, dg in offsets:
        came_from.append((lax.rem(half + 2 - dx, 2), lax.rem(gx + n_gx - dg, n_gx)))
    greet = [peer("gy", d) for d in y_peers] + [who for _, _, who in plane] + [partner]
    barrier = pltpu.get_barrier_semaphore()
    for who in greet:
        pl.semaphore_signal(barrier, inc=1, device_id=who, device_id_type=MESH)
    pl.semaphore_wait(barrier, len(greet))

    mine = pl.ds(pl.multiple_of(gy * rows, rows), rows)

    def send(c, k):
        x, s = c // quarter, c % quarter
        d = y_peers[k]
        return pltpu.make_async_remote_copy(
            src_ref=field.at[x, :, d * quarter + s, :],
            dst_ref=reg.at[c, mine, :],
            send_sem=ssem.at[c, k],
            recv_sem=rsem.at[c, k],
            device_id=peer("gy", d),
            device_id_type=MESH,
        )

    def keep(c):
        x, s = c // quarter, c % quarter
        return pltpu.make_async_copy(
            field.at[x, :, gy * quarter + s, :], reg.at[c, mine, :], lsem.at[c]
        )

    def post(c):
        for k in range(n_gy - 1):
            send(c, k).start()

    for c in range(AHEAD):
        post(c)

    def keep_own(q):
        return pltpu.make_async_copy(
            field.at[q // species, :, q % species, :], own.at[q], osem.at[q]
        )

    @pl.loop(0, own.shape[0])
    def _(q):
        keep_own(q).start()

    @pl.loop(0, chunks)
    def _(c):
        keep(c).start()

    fetch = pltpu.make_async_copy(start, sbuf, bsem.at[0])
    fetch.start()

    def send_more(e, k):
        c = chunks - extra + e
        x, s = c // quarter, c % quarter
        d = y_peers[k]
        return pltpu.make_async_remote_copy(
            src_ref=field.at[x, :, mirror(d) * quarter + s, :],
            dst_ref=xreg.at[e, mine, :],
            send_sem=xssem.at[e, k],
            recv_sem=xrsem.at[e, k],
            device_id=peer("gy", d),
            device_id_type=MESH,
        )

    def keep_more(e):
        c = chunks - extra + e
        x, s = c // quarter, c % quarter
        return pltpu.make_async_copy(
            field.at[x, :, mirror(gy) * quarter + s, :], xreg.at[e, mine, :], xlsem.at[e]
        )

    def start_more(e):
        for k in range(n_gy - 1):
            send_more(e, k).start()
        keep_more(e).start()

    used = [0]

    def swap(src, dst, who):
        s = used[0]
        used[0] += 1
        cp = pltpu.make_async_remote_copy(
            src_ref=src, dst_ref=dst, send_sem=sems.at[0, s], recv_sem=sems.at[1, s],
            device_id=who, device_id_type=MESH,
        )
        cp.start()
        return cp

    def span(at, size):
        return pl.ds(pl.multiple_of(at, 8), size)

    row = lax.broadcasted_iota(jnp.int32, (B, B), 0)
    col = lax.broadcasted_iota(jnp.int32, (B, B), 1)
    eye = jnp.where(row == col, 1.0, 0.0).astype(F32)
    diag[...] = jnp.zeros_like(diag)

    @pl.loop(0, own.shape[0])
    def _(q):
        keep_own(q).wait()
        f = own[q]
        diag[...] += dot3(f, f, 1, 1)

    n_p = 2 * n_gx
    rows_d = part_d.shape[1]
    for p in range(2 * n_p):
        part_d[p] = diag[p * rows_d:(p + 1) * rows_d]
    cp = swap(part_d.at[pl.ds((1 - side) * n_p, n_p)], tmp_dc, partner)
    fetch.wait()
    basis_t[...] = sbuf[...].T
    part[...] = jnp.zeros_like(part)
    r[...] = jnp.zeros_like(r)
    cp.wait()
    for p in range(n_p):
        part_d[side * n_p + p] += tmp_dc[p]
    cps = []
    for k, (h, g, who) in enumerate(plane):
        cps.append(swap(part_d.at[side * n_p + h * n_gx + g], tmp_dg.at[k], who))

    blocks = above(nb)

    def gather(c, more):
        for k in range(n_gy - 1):
            send(c, k).wait_recv()
        if more:
            post(c + AHEAD)
        keep(c).wait()
        fh, fl = pieces(reg[c])
        fcat[c, :, :width] = fh
        fcat[c, :, width:] = fl
        for lo, mid, hi in halvings(0, nb):
            a, z = slice(lo * B, mid * B), slice(mid * B, hi * B)
            res = dotp((fh[a], fl[a]), (fh[z], fl[z]), 1, 1)
            for i in range(lo, mid):
                for j in range(mid, hi):
                    b = blocks.index((i, j))
                    part[b * B:(b + 1) * B, :] += res[
                        (i - lo) * B:(i - lo + 1) * B, (j - mid) * B:(j - mid + 1) * B
                    ]

    def gathers(lo, hi):
        @pl.loop(lo, min(hi, chunks - AHEAD))
        def _(c):
            gather(c, True)

        @pl.loop(max(lo, chunks - AHEAD), hi)
        def _(c):
            gather(c, False)

    gathers(0, 1)
    for cp in cps:
        cp.wait()
    mine_d = side * n_p + half * n_gx + gx
    acc = part_d[mine_d]
    for k in range(len(plane)):
        acc += tmp_dg[k]
    full_d[gy, mine_d] = acc
    cps = []
    for d in y_peers:
        here = full_d.at[gy, mine_d]
        cps.append(swap(here, here, peer("gy", d)))
    gathers(1, 4)
    for cp in cps:
        cp.wait()
    here = full_d.at[:, mine_d]
    plane_d = [swap(here, here, who) for _, _, who in plane]
    onward = [swap(here, here, partner)]
    gathers(4, 5)
    for cp, (h, g) in zip(plane_d, came_from):
        cp.wait()
        here = full_d.at[:, side * n_p + h * n_gx + g]
        onward.append(swap(here, here, partner))
    gathers(5, 6)
    for cp in onward:
        cp.wait()
    for i in range(nb):
        for p in range(2 * n_p):
            there = slice(i * B + p * rows_d, i * B + (p + 1) * rows_d)
            block = full_d[i, p]
            r[there, i * B:(i + 1) * B] = block
    for i in range(nb):
        here = slice(i * B, (i + 1) * B)
        gh[here, here], gl[here, here] = pieces(r[here, here])
    load_block(0, r, m_g, eye)
    factor_blocks([m_g])
    gathers(6, chunks - 1)
    gathers(chunks - 1, chunks)

    total = part.shape[0]
    n_c = total // 2
    n_q = n_c // PARTS
    n_g = n_q // n_p
    keep_c = side * n_c

    def piece(q, h, g):
        return span(keep_c + q * n_q + (h * n_gx + g) * n_g, n_g)

    halves, planes_g, lines, spread = [], [], [], []
    for q in range(PARTS):
        there = span(n_c - keep_c + q * n_q, n_q)
        halves.append(swap(part.at[there, :], tmp_c.at[q], partner))
    for q in range(PARTS):
        halves[q].wait_recv()
        part[span(keep_c + q * n_q, n_q), :] += tmp_c[q]
        planes_g.append([
            swap(part.at[piece(q, h, g), :], tmp_g.at[k, q], who)
            for k, (h, g, who) in enumerate(plane)
        ])
    for q in range(PARTS):
        for cp in planes_g[q]:
            cp.wait_recv()
        mine_g = piece(q, half, gx)
        acc = part[mine_g, :]
        for k in range(len(plane)):
            acc += tmp_g[k, q]
        part[mine_g, :] = acc
        lines.append([
            swap(part.at[mine_g, :], tmp_y.at[k, q], peer("gy", d))
            for k, d in enumerate(y_peers)
        ])
    onward = []
    for q in range(PARTS):
        for cp in lines[q]:
            cp.wait_recv()
        mine_g = piece(q, half, gx)
        acc = part[mine_g, :]
        for k in range(n_gy - 1):
            acc += tmp_y[k, q]
        full[mine_g, :] = acc
        here = full.at[mine_g, :]
        spread.append([swap(here, here, who) for _, _, who in plane])
        onward.append(swap(here, here, partner))
    for e in range(extra):
        start_more(e)
    for q in range(PARTS):
        for cp, (h, g) in zip(spread[q], came_from):
            cp.wait_recv()
            here = full.at[piece(q, h, g), :]
            onward.append(swap(here, here, partner))
    for cp in onward:
        cp.wait_recv()
    sent = halves + sum(planes_g + lines + spread, []) + onward

    for b, (i, j) in enumerate(blocks):
        block = full[b * B:(b + 1) * B, :]
        there = (slice(i * B, (i + 1) * B), slice(j * B, (j + 1) * B))
        bh, bl = pieces(block)
        gh[there], gl[there] = bh, bl
        gh[there[::-1]], gl[there[::-1]] = bh.T, bl.T
        r[there] = block

    def apply_gram():
        return dotp(pieces(basis_t[...]), (gh[...], gl[...]), 1, 0)

    def load_small(wide):
        m_s[:, :B] = dotp(wide, wide, 1, 1)
        m_s[:, B:] = eye

    def small_inverse():
        return pieces(jnp.where(row >= col, m_s[:, B:], 0.0))

    for step in range(ITERS - 1):
        wide = pieces(apply_gram())
        load_small(wide)
        factor_blocks([m_s], [lambda: finish_block(0, r, m_g, row, col)] if step == 0 else [])
        basis_t[...] = dotp(small_inverse(), wide, 1, 0)
    wide = pieces(apply_gram())
    load_small(wide)
    left = jnp.concatenate(wide, axis=0)

    def project(c):
        f = fcat[c]
        res = jnp.dot(left, f, preferred_element_type=F32)
        proj[c] = (res[B:, :width] + res[:B, width:]) + res[:B, :width]

    factor_blocks([m_s], [functools.partial(project, c) for c in range(chunks)])
    inverse = small_inverse()
    cps = []
    used_c = [0]

    def give(c, x, s, d):
        k = used_c[0]
        used_c[0] += 1
        cp = pltpu.make_async_remote_copy(
            src_ref=proj.at[c, span(d * kept, kept), :], dst_ref=core[x].at[:, s, :],
            send_sem=cssem.at[k], recv_sem=crsem.at[k],
            device_id=peer("gy", d), device_id_type=MESH,
        )
        cp.start()
        cps.append(cp)

    for c in range(chunks + extra):
        if c >= chunks:
            e = c - chunks
            for k in range(n_gy - 1):
                send_more(e, k).wait()
            keep_more(e).wait()
            fh, fl = pieces(xreg[e])
            fcat[c, :, :width] = fh
            fcat[c, :, width:] = fl
            project(c)
        own_c = c if c < chunks else c - extra
        x, s = own_c // quarter, own_c % quarter
        s = s + (gy if c < chunks else mirror(gy)) * quarter
        proj[c] = dotp(inverse, pieces(proj[c]), 1, 0)
        for d in (y_peers[1:] + y_peers[:1] if c < chunks - extra else near):
            give(c, x, s, d)
        cp = pltpu.make_async_copy(
            proj.at[c, span(gy * kept, kept), :], core[x].at[:, s, :], clsem.at[c]
        )
        cp.start()
        cps.append(cp)

    load_block(1, r, m_g, eye)
    later = []
    for step in range(1, nb):
        factor_blocks([m_g], later)
        lo, hi = step * B, (step + 1) * B
        r[lo:hi, lo:hi] = jnp.where(row <= col, m_g[:, :B], 0.0)
        if hi < n:
            inv = pieces(jnp.where(row >= col, m_g[:, B:], 0.0))
            u = dotp(inv, pieces(r[lo:hi, hi:]), 1, 0)
            r[lo:hi, hi:] = u
            u = pieces(u)
            first = (u[0][:, :B], u[1][:, :B])
            m_g[:, :B] = r[hi:hi + B, hi:hi + B] - dotp(first, first, 0, 0)
            m_g[:, B:] = eye

            def rest(hi=hi, u=u):
                v = (u[0][:, B:], u[1][:, B:])
                r[hi:, hi + B:] -= dotp(u, v, 0, 0)

            later = [rest] if hi + B < n else []
    scale = 1.0 / jnp.sqrt(F32(columns))
    factor[...] = jnp.zeros_like(factor)
    for i, j in upper(nb):
        @pl.when((gy == j) & (gz == i))
        def _():
            factor[...] = r[i * B:(i + 1) * B, j * B:(j + 1) * B].T * scale
    for cp in cps:
        cp.wait()
    for cp in sent:
        cp.wait_send()

    @pl.loop(0, chunks)
    def _(c):
        for k in range(n_gy - 1):
            send(c, k).wait_send()


def hand_over(*refs):
    *core, factor, core_out, factor_out, sems = refs
    cps = [pltpu.make_async_copy(c, core_out.at[x], sems.at[x]) for x, c in enumerate(core)]
    cps.append(pltpu.make_async_copy(factor, factor_out, sems.at[len(core)]))
    for cp in cps:
        cp.start()
    for cp in cps:
        cp.wait()


def per_device(sizes, field, start_basis):
    n_gx, n_gy, n_gz = sizes
    planes, rows, species, width = field.shape
    n, rank = start_basis.shape
    quarter = species // n_gy
    chunks = planes * quarter
    nb = n // B
    total = len(above(nb)) * B
    columns = planes * n_gx * species * width * n_gz
    n_g = total // 4 // n_gx // PARTS
    others = 2 * n_gx - 1
    n_sems = (1 + PARTS) * (1 + others + (n_gy - 1) + 2 * others + 1)
    rows_d = B // (4 * n_gx)
    held = max(EXTRA, 1)
    n_give = (chunks - EXTRA) * (n_gy - 1) + 2 * EXTRA * (n_gy // 2 - 1)
    dma = pltpu.SemaphoreType.DMA
    outs = (
        jax.ShapeDtypeStruct((planes, rank // n_gy, species, width), F32),
        jax.ShapeDtypeStruct((n // n_gy, n // n_gz), F32),
    )
    *cores, factor = pl.pallas_call(
        functools.partial(kernel, sizes, columns),
        out_shape=[jax.ShapeDtypeStruct(outs[0].shape[1:], F32)] * planes + [outs[1]],
        in_specs=[HBM, HBM],
        out_specs=[VMEM] * (planes + 1),
        scratch_shapes=[
            pltpu.VMEM((chunks, n, width), F32),
            pltpu.VMEM((held, n, width), F32),
            pltpu.VMEM((chunks + EXTRA, n, 2 * width), BF16),
            pltpu.VMEM((planes * species, rows, width), F32),
            pltpu.VMEM((n, rank), F32),
            pltpu.VMEM((rank, n), F32),
            pltpu.VMEM((total, B), F32),
            pltpu.VMEM((PARTS, total // 2 // PARTS, B), F32),
            pltpu.VMEM((others, PARTS, n_g, B), F32),
            pltpu.VMEM((n_gy - 1, PARTS, n_g, B), F32),
            pltpu.VMEM((total, B), F32),
            pltpu.VMEM((B, B), F32),
            pltpu.VMEM((4 * n_gx, rows_d, B), F32),
            pltpu.VMEM((2 * n_gx, rows_d, B), F32),
            pltpu.VMEM((others, rows_d, B), F32),
            pltpu.VMEM((n_gy, 4 * n_gx, rows_d, B), F32),
            pltpu.VMEM((n, n), BF16),
            pltpu.VMEM((n, n), BF16),
            pltpu.VMEM((n, n), F32),
            pltpu.VMEM((B, 2 * B), F32),
            pltpu.VMEM((B, 2 * B), F32),
            pltpu.VMEM((chunks + EXTRA, rank, width), F32),
            dma((2, n_sems)),
            dma((chunks, n_gy - 1)),
            dma((chunks, n_gy - 1)),
            dma((chunks,)),
            dma((held, n_gy - 1)),
            dma((held, n_gy - 1)),
            dma((held,)),
            dma((planes * species,)),
            dma((1,)),
            dma((n_give,)),
            dma((n_give,)),
            dma((chunks + EXTRA,)),
        ],
        compiler_params=pltpu.CompilerParams(
            collective_id=0, has_side_effects=True, vmem_limit_bytes=(53 << 20) + (320 << 10)
        ),
        name="step",
    )(field, start_basis)
    core, factor = pl.pallas_call(
        hand_over,
        out_shape=outs,
        in_specs=[VMEM] * (planes + 1),
        out_specs=(HBM, HBM),
        scratch_shapes=[dma((planes + 1,))],
        compiler_params=pltpu.CompilerParams(vmem_limit_bytes=32 << 20),
        name="out",
    )(*cores, factor)
    return factor, core


def solution(mesh):
    sizes = tuple(mesh.shape[a] for a in ("gx", "gy", "gz"))
    return jax.shard_map(
        functools.partial(per_device, sizes),
        mesh=mesh,
        in_specs=(P("gx", "gy", None, "gz"), P()),
        out_specs=(P("gy", "gz"), P("gx", "gy", None, "gz")),
        check_vma=False,
    )
```
